32 devices in a mesh: groups: 2 (over x), pass: 2 (over core), mp: 8 (over z, y).
Axes of the slice: x: 2, y: 2, z: 4, core: 2. Of those that a mesh axis runs over, the one named last changes fastest.
Arguments:
- passages: bfloat16 [4096, 1024], P(('groups', 'pass', 'mp')), parts along dimension 0, may hold values from -6 to 6
- gain: float32 [1024], replicated, may hold values from 0.1 to 1.9
- w_in: bfloat16 [1024, 65536], P(None, 'mp'), may hold values from -0.1875 to 0.1875
- w_out: bfloat16 [65536, 1024], P('mp'), may hold values from -0.0234375 to 0.0234375
- w_key: bfloat16 [1024, 16384], P(None, 'mp'), may hold values from -0.1875 to 0.1875
- w_value: bfloat16 [1024, 16384], P(None, 'mp'), may hold values from -0.1875 to 0.1875
- queries: bfloat16 [32, 256, 16384], P(('groups', 'pass'), None, 'mp'), parts along dimension 0, may hold values from -72 to 72
- ids: int32 [4096], P('groups'), parts along dimension 0, may hold values from 0 to 4094, as said below
- counts: int32 [32], P(('groups', 'pass')), parts along dimension 0, may hold values from 1 to 255, as said below
Outputs:
- context: bfloat16 [32, 256, 16384], P(('groups', 'pass'), None, 'mp'), parts along dimension 0
The draws below stay inside these ranges and needn't reach their ends.
There are 2 independent parts, one for each index of `groups`. The reference program is written for one: setup_inputs(seed, part) draws one part's arguments, and reference() takes and returns one part's arrays. A program takes and returns all parts, laid end to end along the dimension named above; an argument that names none is the same for every part. Nothing has to cross between parts.
Inputs may be any that keep to these rules, and one draw needn't show every extreme that they name: counts sum to 2048; the last question has exactly 255 passages and some question exactly 1. ids are distinct; ids[r] // 256 is a question q with ids[r] % 256 < counts[q], and every such slot is named by exactly one row.
All inputs are finite; a program needn't handle non-finite values.
Results may differ from the reference program's by a relative error of at most 0.02.
The reference program's roundings to bfloat16 on the way (of `normed`, `hidden`, `encoded`, `slot_rows`, `key_rows`, `value_rows` and `weights`) count: a program that leaves them out, or rounds other values in their place, can miss the bound.
Values may be sent and summed in bfloat16 or wider, within the bound.
A program may use at most 192 MiB of HBM per device.

```python
import jax
import jax.numpy as jnp
from jax import lax

D = 1024
FF = 65536
HEADS = 128
HEAD = 128
MEANP = 128
QUERIES = 256
SLOTS = 256
ROWS = 2048
QUESTIONS = 16
COLS = 16384


def question_layout(key):
    pair_key = jax.random.fold_in(key, 11)
    order_key = jax.random.fold_in(key, 12)
    slot_key = jax.random.fold_in(key, 13)
    pair_count = QUESTIONS // 2
    spread = jax.random.randint(pair_key, (pair_count,), 0, MEANP)
    spread = spread.at[0].set(MEANP - 1)
    paired = jnp.stack([MEANP - spread, MEANP + spread], axis=1)
    others = jax.random.permutation(order_key, paired[1:].reshape(QUESTIONS - 2))
    question_sizes = jnp.concatenate([others, paired[0]], axis=0)
    position = jnp.arange(QUESTIONS * SLOTS) % SLOTS
    owner_index = jnp.arange(QUESTIONS * SLOTS) // SLOTS
    live_slot = position < question_sizes[owner_index]
    rank_order = jax.random.permutation(slot_key, QUESTIONS * SLOTS)
    scored = jnp.where(live_slot, rank_order, rank_order + QUESTIONS * SLOTS)
    chosen = jnp.argsort(scored)[:ROWS]
    return (question_sizes.astype(jnp.int32), chosen.astype(jnp.int32))


def draw_ids(key, part):
    return question_layout(key)[1]


def draw_counts(key, part):
    return question_layout(key)[0]


def draw_queries(key, part):
    base = jnp.clip(jax.random.normal(jax.random.fold_in(key, 21), (QUESTIONS, QUERIES, HEADS * HEAD), jnp.float32), -6.0, 6.0)
    return (0.15 * base).astype(jnp.bfloat16)


def shard_levels(key, shape, cuts, least, top_value):
    def one(dim, shards_of):
        heights = jax.random.uniform(jax.random.fold_in(jax.random.fold_in(key, 6), dim), (shards_of,), jnp.float32, least / len(cuts), top_value / len(cuts))
        return jnp.repeat(jnp.exp(heights), shape[dim] // shards_of).reshape((-1,) + (1,) * (len(shape) - dim - 1))

    loudness = one(*cuts[0])
    for cut in cuts[1:]:
        loudness = loudness * one(*cut)
    return loudness


def gaussian(stream_key, dims, scale, reach, cuts=(), kind=jnp.bfloat16):
    level = shard_levels(stream_key, dims, cuts, -0.22, 0.18) if cuts else 1.0
    drawn = jax.random.normal(stream_key, dims, jnp.float32) * scale * level
    return jnp.minimum(jnp.maximum(drawn, -reach), reach).astype(kind)


def setup_inputs(seed: int = 0, part: int = 0) -> dict:
    streams_of = jax.random.split(jax.random.key(seed), 10)
    part_keys = jax.random.split(jax.random.fold_in(streams_of[9], part), 10)
    passages = gaussian(part_keys[0], (ROWS, D), 1.0, 6.0, ((0, 16),))
    gain = jnp.clip(1.0 + 0.18 * jax.random.normal(streams_of[1], (D,), jnp.float32), 0.1, 1.9)
    w_in = gaussian(streams_of[2], (D, FF), D ** -0.5, 0.1875, ((1, 8),))
    w_out = gaussian(streams_of[3], (FF, D), FF ** -0.5, 0.0234375, ((0, 8),))
    w_key = gaussian(streams_of[4], (D, COLS), D ** -0.5, 0.1875, ((1, 8),))
    w_value = gaussian(streams_of[5], (D, COLS), D ** -0.5, 0.1875, ((1, 8),))
    queries = draw_queries(jax.random.fold_in(jax.random.fold_in(streams_of[9], part), 71), part)
    ids = draw_ids(jax.random.fold_in(jax.random.fold_in(streams_of[9], part), 71), part)
    counts = draw_counts(jax.random.fold_in(jax.random.fold_in(streams_of[9], part), 71), part)
    return dict(passages=passages, gain=gain, w_in=w_in, w_out=w_out, w_key=w_key, w_value=w_value, queries=queries, ids=ids, counts=counts)


def feed_forward(rows, gain, w_in, w_out):
    wide = rows.astype(jnp.float32)
    scale = lax.rsqrt(lax.optimization_barrier(jnp.mean(wide * wide, axis=-1, keepdims=True)) + 1e-06)
    normed = (wide * scale * gain.astype(jnp.float32)).astype(jnp.bfloat16)
    hidden = jax.nn.relu(jnp.dot(normed, w_in, preferred_element_type=jnp.float32)).astype(jnp.bfloat16)
    return jnp.dot(hidden, w_out, preferred_element_type=jnp.float32)

def attend_one(packed):
    asked, key_block, value_block, limit = packed
    asked = asked.reshape(QUERIES, HEADS, HEAD).astype(jnp.float32)
    keyed = key_block.reshape(SLOTS, HEADS, HEAD).astype(jnp.float32)
    valued = value_block.reshape(SLOTS, HEADS, HEAD).astype(jnp.float32)
    scores = jnp.einsum('ihd,jhd->hij', asked, keyed)
    position = jnp.arange(SLOTS, dtype=jnp.int32)
    valid_key = (position < limit)[None, None, :]
    scores = jnp.where(valid_key, scores, -1e+30)
    peak = lax.optimization_barrier(jnp.max(scores, axis=-1, keepdims=True))
    raised = jnp.where(valid_key, jnp.exp(scores - peak), 0.0)
    weights = (raised / lax.optimization_barrier(jnp.sum(raised, axis=-1, keepdims=True))).astype(jnp.bfloat16)
    mixed = jnp.einsum('hij,jhd->ihd', weights.astype(jnp.float32), valued)
    return mixed.reshape(QUERIES, HEADS * HEAD).astype(jnp.bfloat16)

def reference(passages, gain, w_in, w_out, w_key, w_value, queries, ids, counts):
    ffn_out = feed_forward(passages, gain, w_in, w_out)
    encoded = (passages.astype(jnp.float32) + ffn_out).astype(jnp.bfloat16)
    slot_rows = jnp.zeros((QUESTIONS * SLOTS, D), jnp.bfloat16).at[ids].set(encoded)
    key_rows = jnp.dot(slot_rows, w_key, preferred_element_type=jnp.float32).astype(jnp.bfloat16)
    value_rows = jnp.dot(slot_rows, w_value, preferred_element_type=jnp.float32).astype(jnp.bfloat16)
    key_rows = key_rows.reshape(QUESTIONS, SLOTS, HEADS * HEAD)
    value_rows = value_rows.reshape(QUESTIONS, SLOTS, HEADS * HEAD)
    return lax.map(attend_one, (queries, key_rows, value_rows, counts))
```

```python
import functools

import jax
import jax.numpy as jnp
from jax import lax
from jax.experimental import pallas as pl
from jax.experimental.pallas import tpu as pltpu
from jax.sharding import PartitionSpec as P

HEAD = 128
QUERIES = 256
SLOTS = 256
MESH = pl.DeviceIdType.MESH
INNER = 2


def greet(targets):
    barrier = pltpu.get_barrier_semaphore()
    for target in targets:
        pl.semaphore_signal(barrier, inc=1, device_id=target, device_id_type=MESH)
    pl.semaphore_wait(barrier, len(targets))


def push(src, dst, send_sem, recv_sem, target):
    copy = pltpu.make_async_remote_copy(
        src_ref=src, dst_ref=dst, send_sem=send_sem, recv_sem=recv_sem,
        device_id=target, device_id_type=MESH,
    )
    copy.start()
    return copy


def landed(ref, send_sem, recv_sem, target):
    pltpu.make_async_remote_copy(
        src_ref=ref, dst_ref=ref, send_sem=send_sem, recv_sem=recv_sem,
        device_id=target, device_id_type=MESH,
    ).wait_recv()


def place(outer, inner):
    me = lax.axis_index("mp")
    z, y = me // inner, me % inner
    partner = {"mp": z * inner + (1 - y)}
    ahead = [(z + 1 + k) % outer for k in range(outer - 1)]
    behind = [(z + outer - 1 - k) % outer for k in range(outer - 1)]
    return z, y, partner, ahead, behind


def gather_first(outer, rows, own_ref, out_ref, local_sem, zs, zr, ys, yr):
    z, y, partner, ahead, behind = place(outer, INNER)
    greet([partner] + [{"mp": zz * INNER + y} for zz in ahead])

    def block(zz, yy):
        return out_ref.at[pl.ds(pl.multiple_of((zz * INNER + yy) * rows, rows), rows)]

    mine = block(z, y)
    sent = [push(own_ref, mine, ys.at[0], yr.at[0], partner)]
    for k in range(outer - 1):
        sent.append(push(own_ref, mine, zs.at[k], zr.at[k], {"mp": ahead[k] * INNER + y}))
    local = pltpu.make_async_copy(own_ref, mine, local_sem)
    local.start()
    for k in range(outer - 1):
        arrived = block(behind[k], y)
        landed(arrived, zs.at[k], zr.at[k], partner)
        sent.append(push(arrived, arrived, ys.at[k + 1], yr.at[k + 1], partner))
    for k in range(outer):
        zz = z if k == 0 else behind[k - 1]
        arrived = block(zz, 1 - y)
        landed(arrived, ys.at[k], yr.at[k], partner)
    for copy in sent:
        copy.wait_send()
    local.wait()


def all_gather_rows(passages, outer):
    rows, width = passages.shape
    return pl.pallas_call(
        functools.partial(gather_first, outer, rows),
        out_shape=jax.ShapeDtypeStruct((outer * INNER * rows, width), passages.dtype),
        in_specs=[pl.BlockSpec(memory_space=pltpu.VMEM)],
        out_specs=pl.BlockSpec(memory_space=pltpu.VMEM),
        scratch_shapes=[
            pltpu.SemaphoreType.DMA,
            pltpu.SemaphoreType.DMA((outer - 1,)),
            pltpu.SemaphoreType.DMA((outer - 1,)),
            pltpu.SemaphoreType.DMA((outer,)),
            pltpu.SemaphoreType.DMA((outer,)),
        ],
        compiler_params=pltpu.CompilerParams(collective_id=0, has_side_effects=True),
        name="gather_rows",
    )(passages)


def sum_and_share(
    outer, rows, part_ref, own_ref, out_ref,
    from_y, from_z, summed, rys, ryr, rzs, rzr, zs, zr, ys, yr, ps, pr,
):
    z, y, partner, ahead, behind = place(outer, INNER)
    n = outer * INNER
    p = lax.axis_index("pass")
    twin = {"pass": 1 - p}
    peers = [{"mp": zz * INNER + y} for zz in ahead]
    greet([partner, twin] + peers)

    def start(zz, yy):
        return pl.multiple_of((zz * INNER + yy) * rows, rows)

    sent = []
    order = ahead + [z]
    for k in range(outer):
        sent.append(
            push(part_ref.at[pl.ds(start(order[k], 1 - y), rows)], from_y.at[k],
                 rys.at[k], ryr.at[k], partner)
        )
    for k in range(outer - 1):
        sent[k].wait_recv()
        summed[k] = (
            part_ref[pl.ds(start(order[k], y), rows), :].astype(jnp.float32)
            + from_y[k].astype(jnp.float32)
        ).astype(jnp.bfloat16)
        sent.append(push(summed.at[k], from_z.at[k], rzs.at[k], rzr.at[k], peers[k]))
    sent[outer - 1].wait_recv()
    total = part_ref[pl.ds(start(z, y), rows), :].astype(jnp.float32) + from_y[
        outer - 1
    ].astype(jnp.float32)
    for k in range(outer - 1):
        sent[outer + k].wait_recv()
        total += from_z[k].astype(jnp.float32)
    own = pl.multiple_of(p * n * rows + start(z, y), rows)
    out_ref[pl.ds(own, rows), :] = (own_ref[...].astype(jnp.float32) + total).astype(jnp.bfloat16)

    def block(pp, zz, yy):
        return out_ref.at[pl.ds(pl.multiple_of(pp * n * rows + start(zz, yy), rows), rows)]

    mine = block(p, z, y)
    sent.append(push(mine, mine, ys.at[0], yr.at[0], partner))
    for k in range(outer - 1):
        sent.append(push(mine, mine, zs.at[k], zr.at[k], peers[k]))
    sent.append(push(mine, mine, ps.at[0], pr.at[0], twin))
    for k in range(outer):
        if k > 0:
            arrived = block(p, behind[k - 1], y)
            landed(arrived, zs.at[k - 1], zr.at[k - 1], partner)
            sent.append(push(arrived, arrived, ys.at[k], yr.at[k], partner))
            sent.append(push(arrived, arrived, ps.at[k], pr.at[k], twin))
    for k in range(outer):
        arrived = block(p, z if k == 0 else behind[k - 1], 1 - y)
        landed(arrived, ys.at[k], yr.at[k], partner)
        sent.append(push(arrived, arrived, ps.at[outer + k], pr.at[outer + k], twin))
    for k in range(2 * outer):
        kk = k % outer
        arrived = block(1 - p, z if kk == 0 else behind[kk - 1], y if k < outer else 1 - y)
        landed(arrived, ps.at[k], pr.at[k], twin)
    for copy in sent:
        copy.wait_send()


def reduce_and_share(partial, passages, outer):
    rows, width = passages.shape
    n = outer * INNER
    dma = pltpu.SemaphoreType.DMA
    return pl.pallas_call(
        functools.partial(sum_and_share, outer, rows),
        out_shape=jax.ShapeDtypeStruct((2 * n * rows, width), jnp.bfloat16),
        in_specs=[pl.BlockSpec(memory_space=pltpu.VMEM)] * 2,
        out_specs=pl.BlockSpec(memory_space=pltpu.VMEM),
        scratch_shapes=[
            pltpu.VMEM((outer, rows, width), jnp.bfloat16),
            pltpu.VMEM((outer - 1, rows, width), jnp.bfloat16),
            pltpu.VMEM((outer - 1, rows, width), jnp.bfloat16),
            dma((outer,)), dma((outer,)),
            dma((outer - 1,)), dma((outer - 1,)),
            dma((outer - 1,)), dma((outer - 1,)),
            dma((outer,)), dma((outer,)),
            dma((2 * outer,)), dma((2 * outer,)),
        ],
        compiler_params=pltpu.CompilerParams(collective_id=1, has_side_effects=True),
        name="reduce_and_share",
    )(partial, passages)


def attend_kernel(counts_ref, ids_ref, rows_ref, wk_ref, wv_ref, q_ref, o_ref, slot_ref):
    q = pl.program_id(1)

    @pl.when(pl.program_id(0) == 0)
    def _():
        total = ids_ref.shape[1]
        slot_id = lax.broadcasted_iota(jnp.int32, (SLOTS, total), 0) + q * SLOTS
        named = jnp.where(slot_id == ids_ref[...], 1.0, 0.0).astype(jnp.bfloat16)
        slot_ref[q] = jnp.dot(
            named, rows_ref[...], preferred_element_type=jnp.float32
        ).astype(jnp.bfloat16)

    slots = slot_ref[q]
    keyed = jnp.dot(slots, wk_ref[...], preferred_element_type=jnp.float32).astype(jnp.bfloat16)
    valued = jnp.dot(slots, wv_ref[...], preferred_element_type=jnp.float32).astype(jnp.bfloat16)
    valid = lax.broadcasted_iota(jnp.int32, (QUERIES, SLOTS), 1) < counts_ref[q]
    for h in range(wk_ref.shape[1] // HEAD):
        cols = slice(h * HEAD, (h + 1) * HEAD)
        scores = lax.dot_general(
            q_ref[0, :, cols], keyed[:, cols], (((1,), (1,)), ((), ())),
            preferred_element_type=jnp.float32,
        )
        scores = jnp.where(valid, scores, -1e30)
        peak = jnp.max(scores, axis=-1, keepdims=True)
        raised = jnp.where(valid, jnp.exp(scores - peak), 0.0)
        weights = (raised * (1.0 / jnp.sum(raised, axis=-1, keepdims=True))).astype(jnp.bfloat16)
        o_ref[0, :, cols] = jnp.dot(
            weights, valued[:, cols], preferred_element_type=jnp.float32
        ).astype(jnp.bfloat16)


def attend(counts, shifted, all_rows, w_key, w_value, queries):
    questions, asked, cols = queries.shape
    total, width = all_rows.shape
    step = min(cols, 8 * HEAD)
    while cols % step:
        step -= HEAD
    return pl.pallas_call(
        attend_kernel,
        out_shape=jax.ShapeDtypeStruct(queries.shape, jnp.bfloat16),
        grid_spec=pltpu.PrefetchScalarGridSpec(
            num_scalar_prefetch=1,
            grid=(cols // step, questions),
            in_specs=[
                pl.BlockSpec((1, total), lambda c, q, s: (0, 0)),
                pl.BlockSpec((total, width), lambda c, q, s: (0, 0)),
                pl.BlockSpec((width, step), lambda c, q, s: (0, c)),
                pl.BlockSpec((width, step), lambda c, q, s: (0, c)),
                pl.BlockSpec((1, asked, step), lambda c, q, s: (q, 0, c)),
            ],
            out_specs=pl.BlockSpec((1, asked, step), lambda c, q, s: (q, 0, c)),
            scratch_shapes=[pltpu.VMEM((questions, SLOTS, width), jnp.bfloat16)],
        ),
        compiler_params=pltpu.CompilerParams(vmem_limit_bytes=56 * 1024 * 1024),
        name="attend",
    )(counts, shifted, all_rows, w_key, w_value, queries)


def feed_forward(row_block, gain, w_in, w_out):
    wide = row_block.astype(jnp.float32)
    scale = lax.rsqrt(jnp.mean(wide * wide, axis=-1, keepdims=True) + 1e-06)
    normed = (wide * scale * gain).astype(jnp.bfloat16)
    hidden = jax.nn.relu(jnp.dot(normed, w_in, preferred_element_type=jnp.float32)).astype(
        jnp.bfloat16
    )
    return jnp.dot(hidden, w_out, preferred_element_type=jnp.float32).astype(jnp.bfloat16)


def per_device(devices, passages, gain, w_in, w_out, w_key, w_value, queries, ids, counts):
    outer = devices // INNER
    gathered = all_gather_rows(passages, outer)
    partial = feed_forward(gathered, gain, w_in, w_out)
    all_rows = reduce_and_share(partial, passages, outer)
    slot_total = counts.shape[0] * SLOTS
    shifted = (ids - lax.axis_index("pass") * slot_total)[None, :]
    return attend(counts, shifted, all_rows, w_key, w_value, queries)


def solution(mesh):
    placed = (
        P(("groups", "pass", "mp"), None),
        P(),
        P(None, "mp"),
        P("mp", None),
        P(None, "mp"),
        P(None, "mp"),
        P(("groups", "pass"), None, "mp"),
        P("groups"),
        P(("groups", "pass")),
    )
    return jax.shard_map(
        functools.partial(per_device, mesh.shape["mp"]),
        mesh=mesh,
        in_specs=placed,
        out_specs=P(("groups", "pass"), None, "mp"),
        check_vma=False,
    )
```

```python
import functools

import jax
import jax.numpy as jnp
from jax import lax
from jax.experimental import pallas as pl
from jax.experimental.pallas import tpu as pltpu
from jax.sharding import PartitionSpec as P

HEAD = 128
QUERIES = 256
SLOTS = 256
MESH = pl.DeviceIdType.MESH
INNER = 2


def greet(targets):
    barrier = pltpu.get_barrier_semaphore()
    for target in targets:
        pl.semaphore_signal(barrier, inc=1, device_id=target, device_id_type=MESH)
    pl.semaphore_wait(barrier, len(targets))


def push(src, dst, send_sem, recv_sem, target):
    copy = pltpu.make_async_remote_copy(
        src_ref=src, dst_ref=dst, send_sem=send_sem, recv_sem=recv_sem,
        device_id=target, device_id_type=MESH,
    )
    copy.start()
    return copy


def landed(ref, send_sem, recv_sem, target):
    pltpu.make_async_remote_copy(
        src_ref=ref, dst_ref=ref, send_sem=send_sem, recv_sem=recv_sem,
        device_id=target, device_id_type=MESH,
    ).wait_recv()


def gone(ref, send_sem, recv_sem, target):
    pltpu.make_async_remote_copy(
        src_ref=ref, dst_ref=ref, send_sem=send_sem, recv_sem=recv_sem,
        device_id=target, device_id_type=MESH,
    ).wait_send()


def place(outer, inner):
    me = lax.axis_index("mp")
    z, y = me // inner, me % inner
    partner = {"mp": z * inner + (1 - y)}
    ahead = [(z + 1 + k) % outer for k in range(outer - 1)]
    behind = [(z + outer - 1 - k) % outer for k in range(outer - 1)]
    return z, y, partner, ahead, behind


def encode_kernel(
    outer, rows, chunk, own_ref, gain_ref, w_in_ref, w_out_ref, out_ref,
    gathered, w_in_here, w_out_here, normed, total, parts, from_y, from_z, summed,
    in_sem, out_sem, local_sem, gzs, gzr, gys, gyr, rys, ryr, rzs, rzr, zs, zr, ys, yr, ps, pr,
):
    z, y, partner, ahead, behind = place(outer, INNER)
    n = outer * INNER
    chunks = w_in_here.shape[0]
    p = lax.axis_index("pass")
    twin = {"pass": 1 - p}

    def load_in(c):
        cols = pl.ds(pl.multiple_of(c * chunk, chunk), chunk)
        return pltpu.make_async_copy(w_in_ref.at[:, cols], w_in_here.at[c], in_sem.at[c])

    def load_out(c):
        cols = pl.ds(pl.multiple_of(c * chunk, chunk), chunk)
        return pltpu.make_async_copy(w_out_ref.at[cols, :], w_out_here.at[c], out_sem.at[c])

    for c in range(chunks):
        load_in(c).start()
        load_out(c).start()
    greet([partner, twin] + [{"mp": zz * INNER + y} for zz in ahead])

    def start(zz, yy):
        return pl.multiple_of((zz * INNER + yy) * rows, rows)

    def held(zz, yy):
        return gathered.at[pl.ds(start(zz, yy), rows)]

    push(own_ref, held(z, y), gys.at[0], gyr.at[0], partner)
    for k in range(outer - 1):
        push(own_ref, held(z, y), gzs.at[k], gzr.at[k], {"mp": ahead[k] * INNER + y})
    local = pltpu.make_async_copy(own_ref, held(z, y), local_sem)
    local.start()
    local.wait()

    def add_pair(k):
        landed(from_y.at[k], rys.at[k], ryr.at[k], partner)
        here = parts[k, pl.ds(pl.multiple_of(y * rows, rows), rows), :]
        summed[k - 1] = (
            here.astype(jnp.float32) + from_y[k].astype(jnp.float32)
        ).astype(jnp.bfloat16)
        owner = (z + outer - k) % outer
        push(summed.at[k - 1], from_z.at[k - 1], rzs.at[k - 1], rzr.at[k - 1],
             {"mp": owner * INNER + y})

    def group(k, carry):
        zz = (z + outer - k) % outer
        landed(held(zz, 1 - y), gys.at[k], gyr.at[k], partner)
        wide = gathered[pl.ds(start(zz, 0), INNER * rows), :].astype(jnp.float32)
        scale = lax.rsqrt(jnp.mean(wide * wide, axis=-1, keepdims=True) + 1e-06)
        normed[...] = (wide * scale * gain_ref[...]).astype(jnp.bfloat16)
        total[...] = jnp.zeros_like(total)

        def piece(c, carry):
            @pl.when(k == 0)
            def _():
                load_in(c).wait()
                load_out(c).wait()

            hidden = jnp.maximum(
                jnp.dot(normed[...], w_in_here[c], preferred_element_type=jnp.float32), 0.0
            ).astype(jnp.bfloat16)
            total[...] += jnp.dot(hidden, w_out_here[c], preferred_element_type=jnp.float32)

            @pl.when((c == (chunks - 1) // 2) & (k < outer - 1))
            def _():
                later = held((z + outer - k - 1) % outer, y)
                landed(later, gzs.at[k], gzr.at[k], partner)
                push(later, later, gys.at[k + 1], gyr.at[k + 1], partner)

            @pl.when((c == (chunks - 1) // 2) & (k > 1))
            def _():
                add_pair(k - 1)

            return carry

        lax.fori_loop(0, chunks, piece, 0)
        parts[k] = total[...].astype(jnp.bfloat16)
        push(parts.at[k, pl.ds(pl.multiple_of((1 - y) * rows, rows), rows)], from_y.at[k],
             rys.at[k], ryr.at[k], partner)
        return carry

    lax.fori_loop(0, outer, group, 0)
    add_pair(outer - 1)
    landed(from_y.at[0], rys.at[0], ryr.at[0], partner)
    mine = pl.ds(pl.multiple_of(y * rows, rows), rows)
    ffn = parts[0, mine, :].astype(jnp.float32) + from_y[0].astype(jnp.float32)
    for k in range(outer - 1):
        landed(from_z.at[k], rzs.at[k], rzr.at[k], partner)
        ffn += from_z[k].astype(jnp.float32)
    own = pl.multiple_of(p * n * rows + start(z, y), rows)
    out_ref[pl.ds(own, rows), :] = (own_ref[...].astype(jnp.float32) + ffn).astype(jnp.bfloat16)

    def block(pp, zz, yy):
        return out_ref.at[pl.ds(pl.multiple_of(pp * n * rows + start(zz, yy), rows), rows)]

    mine = block(p, z, y)
    sent = [push(mine, mine, ys.at[0], yr.at[0], partner)]
    for k in range(outer - 1):
        sent.append(push(mine, mine, zs.at[k], zr.at[k], {"mp": ahead[k] * INNER + y}))
    sent.append(push(mine, mine, ps.at[0], pr.at[0], twin))
    for k in range(1, outer):
        arrived = block(p, behind[k - 1], y)
        landed(arrived, zs.at[k - 1], zr.at[k - 1], partner)
        sent.append(push(arrived, arrived, ys.at[k], yr.at[k], partner))
        sent.append(push(arrived, arrived, ps.at[k], pr.at[k], twin))
    for k in range(outer):
        arrived = block(p, z if k == 0 else behind[k - 1], 1 - y)
        landed(arrived, ys.at[k], yr.at[k], partner)
        sent.append(push(arrived, arrived, ps.at[outer + k], pr.at[outer + k], twin))
    for k in range(2 * outer):
        kk = k % outer
        arrived = block(1 - p, z if kk == 0 else behind[kk - 1], y if k < outer else 1 - y)
        landed(arrived, ps.at[k], pr.at[k], twin)
    for copy in sent:
        copy.wait_send()
    for k in range(outer):
        gone(held(z, y), gys.at[k], gyr.at[k], partner)
        gone(from_y.at[k], rys.at[k], ryr.at[k], partner)
    for k in range(outer - 1):
        gone(held(z, y), gzs.at[k], gzr.at[k], partner)
        gone(summed.at[k], rzs.at[k], rzr.at[k], partner)


def encode(passages, gain, w_in, w_out, outer):
    rows, width = passages.shape
    n = outer * INNER
    units = w_in.shape[1]
    chunk = min(units, 1024)
    while units % chunk:
        chunk -= 128
    chunks = units // chunk
    dma = pltpu.SemaphoreType.DMA
    vmem = pl.BlockSpec(memory_space=pltpu.VMEM)
    hbm = pl.BlockSpec(memory_space=pl.ANY)
    bf16 = jnp.bfloat16
    return pl.pallas_call(
        functools.partial(encode_kernel, outer, rows, chunk),
        out_shape=jax.ShapeDtypeStruct((2 * n * rows, width), bf16),
        in_specs=[vmem, vmem, hbm, hbm],
        out_specs=vmem,
        scratch_shapes=[
            pltpu.VMEM((n * rows, width), bf16),
            pltpu.VMEM((chunks, width, chunk), bf16),
            pltpu.VMEM((chunks, chunk, width), bf16),
            pltpu.VMEM((INNER * rows, width), bf16),
            pltpu.VMEM((INNER * rows, width), jnp.float32),
            pltpu.VMEM((outer, INNER * rows, width), bf16),
            pltpu.VMEM((outer, rows, width), bf16),
            pltpu.VMEM((outer - 1, rows, width), bf16),
            pltpu.VMEM((outer - 1, rows, width), bf16),
            dma((chunks,)), dma((chunks,)), dma,
            dma((outer - 1,)), dma((outer - 1,)), dma((outer,)), dma((outer,)),
            dma((outer,)), dma((outer,)), dma((outer - 1,)), dma((outer - 1,)),
            dma((outer - 1,)), dma((outer - 1,)), dma((outer,)), dma((outer,)),
            dma((2 * outer,)), dma((2 * outer,)),
        ],
        compiler_params=pltpu.CompilerParams(
            collective_id=0, has_side_effects=True, vmem_limit_bytes=60 * 1024 * 1024
        ),
        name="encode",
    )(passages, gain[None, :], w_in, w_out)


def attend_kernel(counts_ref, ids_ref, rows_ref, wk_ref, wv_ref, q_ref, o_ref, slot_ref):
    q = pl.program_id(1)

    @pl.when(pl.program_id(0) == 0)
    def _():
        total = ids_ref.shape[1]
        slot_id = lax.broadcasted_iota(jnp.int32, (SLOTS, total), 0) + q * SLOTS
        named = jnp.where(slot_id == ids_ref[...], 1.0, 0.0).astype(jnp.bfloat16)
        slot_ref[q] = jnp.dot(
            named, rows_ref[...], preferred_element_type=jnp.float32
        ).astype(jnp.bfloat16)

    slots = slot_ref[q]
    keyed = jnp.dot(slots, wk_ref[...], preferred_element_type=jnp.float32).astype(jnp.bfloat16)
    valued = jnp.dot(slots, wv_ref[...], preferred_element_type=jnp.float32).astype(jnp.bfloat16)
    valid = lax.broadcasted_iota(jnp.int32, (QUERIES, SLOTS), 1) < counts_ref[q]
    for h in range(wk_ref.shape[1] // HEAD):
        cols = slice(h * HEAD, (h + 1) * HEAD)
        scores = lax.dot_general(
            q_ref[0, :, cols], keyed[:, cols], (((1,), (1,)), ((), ())),
            preferred_element_type=jnp.float32,
        )
        scores = jnp.where(valid, scores, -1e30)
        peak = jnp.max(scores, axis=-1, keepdims=True)
        raised = jnp.where(valid, jnp.exp(scores - peak), 0.0)
        weights = (raised * (1.0 / jnp.sum(raised, axis=-1, keepdims=True))).astype(jnp.bfloat16)
        o_ref[0, :, cols] = jnp.dot(
            weights, valued[:, cols], preferred_element_type=jnp.float32
        ).astype(jnp.bfloat16)


def attend(counts, shifted, all_rows, w_key, w_value, queries):
    questions, asked, cols = queries.shape
    total, width = all_rows.shape
    step = min(cols, 8 * HEAD)
    while cols % step:
        step -= HEAD
    return pl.pallas_call(
        attend_kernel,
        out_shape=jax.ShapeDtypeStruct(queries.shape, jnp.bfloat16),
        grid_spec=pltpu.PrefetchScalarGridSpec(
            num_scalar_prefetch=1,
            grid=(cols // step, questions),
            in_specs=[
                pl.BlockSpec((1, total), lambda c, q, s: (0, 0)),
                pl.BlockSpec((total, width), lambda c, q, s: (0, 0)),
                pl.BlockSpec((width, step), lambda c, q, s: (0, c)),
                pl.BlockSpec((width, step), lambda c, q, s: (0, c)),
                pl.BlockSpec((1, asked, step), lambda c, q, s: (q, 0, c)),
            ],
            out_specs=pl.BlockSpec((1, asked, step), lambda c, q, s: (q, 0, c)),
            scratch_shapes=[pltpu.VMEM((questions, SLOTS, width), jnp.bfloat16)],
        ),
        compiler_params=pltpu.CompilerParams(vmem_limit_bytes=56 * 1024 * 1024),
        name="attend",
    )(counts, shifted, all_rows, w_key, w_value, queries)


def per_device(devices, passages, gain, w_in, w_out, w_key, w_value, queries, ids, counts):
    outer = devices // INNER
    all_rows = encode(passages, gain, w_in, w_out, outer)
    slot_total = counts.shape[0] * SLOTS
    shifted = (ids - lax.axis_index("pass") * slot_total)[None, :]
    return attend(counts, shifted, all_rows, w_key, w_value, queries)


def solution(mesh):
    placed = (
        P(("groups", "pass", "mp"), None),
        P(),
        P(None, "mp"),
        P("mp", None),
        P(None, "mp"),
        P(None, "mp"),
        P(("groups", "pass"), None, "mp"),
        P("groups"),
        P(("groups", "pass")),
    )
    return jax.shard_map(
        functools.partial(per_device, mesh.shape["mp"]),
        mesh=mesh,
        in_specs=placed,
        out_specs=P(("groups", "pass"), None, "mp"),
        check_vma=False,
    )
```

```python
import functools

import jax
import jax.numpy as jnp
from jax import lax
from jax.experimental import pallas as pl
from jax.experimental.pallas import tpu as pltpu
from jax.sharding import PartitionSpec as P

HEAD = 128
QUERIES = 256
SLOTS = 256
MESH = pl.DeviceIdType.MESH
INNER = 2
ALIGN = 16


def greet(targets):
    barrier = pltpu.get_barrier_semaphore()
    for target in targets:
        pl.semaphore_signal(barrier, inc=1, device_id=target, device_id_type=MESH)
    pl.semaphore_wait(barrier, len(targets))


def push(src, dst, send_sem, recv_sem, target):
    copy = pltpu.make_async_remote_copy(
        src_ref=src, dst_ref=dst, send_sem=send_sem, recv_sem=recv_sem,
        device_id=target, device_id_type=MESH,
    )
    copy.start()
    return copy


def landed(ref, send_sem, recv_sem, target):
    pltpu.make_async_remote_copy(
        src_ref=ref, dst_ref=ref, send_sem=send_sem, recv_sem=recv_sem,
        device_id=target, device_id_type=MESH,
    ).wait_recv()


def gone(ref, send_sem, recv_sem, target):
    pltpu.make_async_remote_copy(
        src_ref=ref, dst_ref=ref, send_sem=send_sem, recv_sem=recv_sem,
        device_id=target, device_id_type=MESH,
    ).wait_send()


def place(outer, inner):
    me = lax.axis_index("mp")
    z, y = me // inner, me % inner
    partner = {"mp": z * inner + (1 - y)}
    ahead = [(z + 1 + k) % outer for k in range(outer - 1)]
    behind = [(z + outer - 1 - k) % outer for k in range(outer - 1)]
    return z, y, partner, ahead, behind


def encode_kernel(
    outer, rows, chunk, own_ref, gain_ref, w_in_ref, w_out_ref, out_ref,
    gathered, w_in_here, w_out_here, normed, total, parts, from_y, from_z, summed,
    in_sem, out_sem, local_sem, gzs, gzr, gys, gyr, rys, ryr, rzs, rzr, zs, zr, ys, yr, ps, pr,
):
    z, y, partner, ahead, behind = place(outer, INNER)
    n = outer * INNER
    chunks = w_in_here.shape[0]
    p = lax.axis_index("pass")
    twin = {"pass": 1 - p}

    def load_in(c):
        cols = pl.ds(pl.multiple_of(c * chunk, chunk), chunk)
        return pltpu.make_async_copy(w_in_ref.at[:, cols], w_in_here.at[c], in_sem.at[c])

    def load_out(c):
        cols = pl.ds(pl.multiple_of(c * chunk, chunk), chunk)
        return pltpu.make_async_copy(w_out_ref.at[cols, :], w_out_here.at[c], out_sem.at[c])

    for c in range(chunks):
        load_in(c).start()
        load_out(c).start()
    greet([partner, twin] + [{"mp": zz * INNER + y} for zz in ahead])

    def start(zz, yy):
        return pl.multiple_of((zz * INNER + yy) * rows, rows)

    def held(zz, yy):
        return gathered.at[pl.ds(start(zz, yy), rows)]

    push(own_ref, held(z, y), gys.at[0], gyr.at[0], partner)
    for k in range(outer - 1):
        push(own_ref, held(z, y), gzs.at[k], gzr.at[k], {"mp": ahead[k] * INNER + y})
    local = pltpu.make_async_copy(own_ref, held(z, y), local_sem)
    local.start()
    local.wait()

    def add_pair(k):
        landed(from_y.at[k], rys.at[k], ryr.at[k], partner)
        here = parts[k, pl.ds(pl.multiple_of(y * rows, rows), rows), :]
        summed[k - 1] = (
            here.astype(jnp.float32) + from_y[k].astype(jnp.float32)
        ).astype(jnp.bfloat16)
        owner = (z + outer - k) % outer
        push(summed.at[k - 1], from_z.at[k - 1], rzs.at[k - 1], rzr.at[k - 1],
             {"mp": owner * INNER + y})

    def group(k, carry):
        zz = (z + outer - k) % outer
        landed(held(zz, 1 - y), gys.at[k], gyr.at[k], partner)
        wide = gathered[pl.ds(start(zz, 0), INNER * rows), :].astype(jnp.float32)
        scale = lax.rsqrt(jnp.mean(wide * wide, axis=-1, keepdims=True) + 1e-06)
        normed[...] = (wide * scale * gain_ref[...]).astype(jnp.bfloat16)
        total[...] = jnp.zeros_like(total)

        def piece(c, carry):
            @pl.when(k == 0)
            def _():
                load_in(c).wait()
                load_out(c).wait()

            hidden = jnp.maximum(
                jnp.dot(normed[...], w_in_here[c], preferred_element_type=jnp.float32), 0.0
            ).astype(jnp.bfloat16)
            total[...] += jnp.dot(hidden, w_out_here[c], preferred_element_type=jnp.float32)

            @pl.when((c == (chunks - 1) // 2) & (k < outer - 1))
            def _():
                later = held((z + outer - k - 1) % outer, y)
                landed(later, gzs.at[k], gzr.at[k], partner)
                push(later, later, gys.at[k + 1], gyr.at[k + 1], partner)

            @pl.when((c == (chunks - 1) // 2) & (k > 1))
            def _():
                add_pair(k - 1)

            return carry

        lax.fori_loop(0, chunks, piece, 0)
        parts[k] = total[...].astype(jnp.bfloat16)
        push(parts.at[k, pl.ds(pl.multiple_of((1 - y) * rows, rows), rows)], from_y.at[k],
             rys.at[k], ryr.at[k], partner)
        return carry

    lax.fori_loop(0, outer, group, 0)
    add_pair(outer - 1)
    landed(from_y.at[0], rys.at[0], ryr.at[0], partner)
    mine = pl.ds(pl.multiple_of(y * rows, rows), rows)
    ffn = parts[0, mine, :].astype(jnp.float32) + from_y[0].astype(jnp.float32)
    for k in range(outer - 1):
        landed(from_z.at[k], rzs.at[k], rzr.at[k], partner)
        ffn += from_z[k].astype(jnp.float32)
    own = pl.multiple_of(p * n * rows + start(z, y), rows)
    out_ref[pl.ds(own, rows), :] = (own_ref[...].astype(jnp.float32) + ffn).astype(jnp.bfloat16)

    def block(pp, zz, yy):
        return out_ref.at[pl.ds(pl.multiple_of(pp * n * rows + start(zz, yy), rows), rows)]

    def spread(zz):
        here = block(p, zz, y)
        push(here, here, ys.at[zz], yr.at[zz], partner)
        push(here, here, ps.at[zz * INNER + y], pr.at[zz * INNER + y], twin)

    def relay(zz, s, side, on, keep):
        @pl.when(keep)
        def _():
            here = block(p, zz, y)
            if s > 0:
                landed(here, zs.at[side, s - 1], zr.at[side, s - 1], partner)
            following = z + 1 if side == 0 else z - 1

            @pl.when(on)
            def _():
                push(here, here, zs.at[side, s], zr.at[side, s], {"mp": following * INNER + y})

            if s > 0:
                spread(zz)

    upward, downward = z < outer - 1, z > 0
    for s in range(outer):
        relay(z - s, s, 0, upward, z - s >= 0)
        relay(z + s, s, 1, downward, z + s < outer)
        if s == 0:
            spread(z)

    def cross(zz, keep):
        @pl.when(keep)
        def _():
            here = block(p, zz, 1 - y)
            landed(here, ys.at[zz], yr.at[zz], partner)
            at = zz * INNER + 1 - y
            push(here, here, ps.at[at], pr.at[at], twin)

    cross(z, z >= 0)
    for s in range(1, outer):
        cross(z - s, z - s >= 0)
        cross(z + s, z + s < outer)
    for k in range(n):
        landed(block(1 - p, k // INNER, k % INNER), ps.at[k], pr.at[k], twin)
    for k in range(n):
        gone(block(p, z, y), ps.at[k], pr.at[k], twin)
    for k in range(outer):
        gone(block(p, z, y), ys.at[k], yr.at[k], partner)

        @pl.when(upward & (z - k >= 0))
        def _():
            gone(block(p, z, y), zs.at[0, k], zr.at[0, k], partner)

        @pl.when(downward & (z + k < outer))
        def _():
            gone(block(p, z, y), zs.at[1, k], zr.at[1, k], partner)

    for k in range(outer):
        gone(held(z, y), gys.at[k], gyr.at[k], partner)
        gone(from_y.at[k], rys.at[k], ryr.at[k], partner)
    for k in range(outer - 1):
        gone(held(z, y), gzs.at[k], gzr.at[k], partner)
        gone(summed.at[k], rzs.at[k], rzr.at[k], partner)


def encode(passages, gain, w_in, w_out, outer):
    rows, width = passages.shape
    n = outer * INNER
    units = w_in.shape[1]
    chunk = min(units, 1024)
    while units % chunk:
        chunk -= 128
    chunks = units // chunk
    dma = pltpu.SemaphoreType.DMA
    vmem = pl.BlockSpec(memory_space=pltpu.VMEM)
    hbm = pl.BlockSpec(memory_space=pl.ANY)
    bf16 = jnp.bfloat16
    return pl.pallas_call(
        functools.partial(encode_kernel, outer, rows, chunk),
        out_shape=jax.ShapeDtypeStruct((2 * n * rows, width), bf16),
        in_specs=[vmem, vmem, hbm, hbm],
        out_specs=vmem,
        scratch_shapes=[
            pltpu.VMEM((n * rows, width), bf16),
            pltpu.VMEM((chunks, width, chunk), bf16),
            pltpu.VMEM((chunks, chunk, width), bf16),
            pltpu.VMEM((INNER * rows, width), bf16),
            pltpu.VMEM((INNER * rows, width), jnp.float32),
            pltpu.VMEM((outer, INNER * rows, width), bf16),
            pltpu.VMEM((outer, rows, width), bf16),
            pltpu.VMEM((outer - 1, rows, width), bf16),
            pltpu.VMEM((outer - 1, rows, width), bf16),
            dma((chunks,)), dma((chunks,)), dma,
            dma((outer - 1,)), dma((outer - 1,)), dma((outer,)), dma((outer,)),
            dma((outer,)), dma((outer,)), dma((outer - 1,)), dma((outer - 1,)),
            dma((2, outer)), dma((2, outer)), dma((outer,)), dma((outer,)),
            dma((n,)), dma((n,)),
        ],
        compiler_params=pltpu.CompilerParams(
            collective_id=0, has_side_effects=True, vmem_limit_bytes=60 * 1024 * 1024
        ),
        name="encode",
    )(passages, gain[None, :], w_in, w_out)


def attend_kernel(
    counts_ref, ids_ref, rows_ref, wk_ref, wv_ref, q_ref, o_ref, slot_ref, key_ref, value_ref
):
    q = pl.program_id(1)
    first = pl.program_id(0) == 0
    questions = counts_ref.shape[0]
    offset, own_offset = [jnp.int32(0)], jnp.int32(0)
    for j in range(questions):
        room = (counts_ref[j] + ALIGN - 1) // ALIGN * ALIGN
        own_offset += jnp.where(j < q, room, 0)
        offset.append(offset[-1] + room)
    own_offset = pl.multiple_of(own_offset, ALIGN)

    @pl.when(q == 0)
    def _():
        tiles = (offset[questions] + SLOTS - 1) // SLOTS

        def tile(t, carry):
            here = pl.ds(pl.multiple_of(t * SLOTS, SLOTS), SLOTS)

            @pl.when(first)
            def _():
                ids = ids_ref[...]
                packed = jnp.full_like(ids, -1)
                for j in range(questions):
                    mine = (ids >= j * SLOTS) & (ids < (j + 1) * SLOTS)
                    packed = jnp.where(mine, ids - j * SLOTS + offset[j], packed)
                line = lax.broadcasted_iota(jnp.int32, (SLOTS, ids.shape[1]), 0) + t * SLOTS
                named = jnp.where(line == packed, 1.0, 0.0).astype(jnp.bfloat16)
                slot_ref[here, :] = jnp.dot(
                    named, rows_ref[...], preferred_element_type=jnp.float32
                ).astype(jnp.bfloat16)

            slots = slot_ref[here, :]
            key_ref[here, :] = jnp.dot(
                slots, wk_ref[...], preferred_element_type=jnp.float32
            ).astype(jnp.bfloat16)
            value_ref[here, :] = jnp.dot(
                slots, wv_ref[...], preferred_element_type=jnp.float32
            ).astype(jnp.bfloat16)
            return carry

        lax.fori_loop(0, tiles, tile, 0)
        tail = pl.ds(pl.multiple_of(tiles * SLOTS, SLOTS), SLOTS)
        value_ref[tail, :] = jnp.zeros((SLOTS, value_ref.shape[1]), jnp.bfloat16)

    def mix(width):
        valid = lax.broadcasted_iota(jnp.int32, (QUERIES, width), 1) < counts_ref[q]
        for h in range(wk_ref.shape[1] // HEAD):
            cols = slice(h * HEAD, (h + 1) * HEAD)
            scores = lax.dot_general(
                q_ref[0, :, cols], key_ref[pl.ds(own_offset, width), cols],
                (((1,), (1,)), ((), ())), preferred_element_type=jnp.float32,
            )
            scores = jnp.where(valid, scores, -1e30)
            peak = jnp.max(scores, axis=-1, keepdims=True)
            raised = jnp.where(valid, jnp.exp(scores - peak), 0.0)
            share = 1.0 / jnp.sum(raised, axis=-1, keepdims=True)
            o_ref[0, :, cols] = jnp.dot(
                (raised * share).astype(jnp.bfloat16),
                value_ref[pl.ds(own_offset, width), cols],
                preferred_element_type=jnp.float32,
            ).astype(jnp.bfloat16)

    few = counts_ref[q] <= SLOTS // 2

    @pl.when(few)
    def _():
        mix(SLOTS // 2)

    @pl.when(jnp.logical_not(few))
    def _():
        mix(SLOTS)


def attend(counts, shifted, all_rows, w_key, w_value, queries):
    questions, asked, cols = queries.shape
    total, width = all_rows.shape
    step = min(cols, 8 * HEAD)
    while cols % step:
        step -= HEAD
    return pl.pallas_call(
        attend_kernel,
        out_shape=jax.ShapeDtypeStruct(queries.shape, jnp.bfloat16),
        grid_spec=pltpu.PrefetchScalarGridSpec(
            num_scalar_prefetch=1,
            grid=(cols // step, questions),
            in_specs=[
                pl.BlockSpec((1, total), lambda c, q, s: (0, 0)),
                pl.BlockSpec((total, width), lambda c, q, s: (0, 0)),
                pl.BlockSpec((width, step), lambda c, q, s: (0, c)),
                pl.BlockSpec((width, step), lambda c, q, s: (0, c)),
                pl.BlockSpec((1, asked, step), lambda c, q, s: (q, 0, c)),
            ],
            out_specs=pl.BlockSpec((1, asked, step), lambda c, q, s: (q, 0, c)),
            scratch_shapes=[
                pltpu.VMEM((questions * SLOTS, width), jnp.bfloat16),
                pltpu.VMEM((questions * SLOTS + SLOTS, step), jnp.bfloat16),
                pltpu.VMEM((questions * SLOTS + SLOTS, step), jnp.bfloat16),
            ],
        ),
        compiler_params=pltpu.CompilerParams(vmem_limit_bytes=56 * 1024 * 1024),
        name="attend",
    )(counts, shifted, all_rows, w_key, w_value, queries)


def per_device(devices, passages, gain, w_in, w_out, w_key, w_value, queries, ids, counts):
    outer = devices // INNER
    all_rows = encode(passages, gain, w_in, w_out, outer)
    slot_total = counts.shape[0] * SLOTS
    shifted = (ids - lax.axis_index("pass") * slot_total)[None, :]
    return attend(counts, shifted, all_rows, w_key, w_value, queries)


def solution(mesh):
    placed = (
        P(("groups", "pass", "mp"), None),
        P(),
        P(None, "mp"),
        P("mp", None),
        P(None, "mp"),
        P(None, "mp"),
        P(("groups", "pass"), None, "mp"),
        P("groups"),
        P(("groups", "pass")),
    )
    return jax.shard_map(
        functools.partial(per_device, mesh.shape["mp"]),
        mesh=mesh,
        in_specs=placed,
        out_specs=P(("groups", "pass"), None, "mp"),
        check_vma=False,
    )
```

```python
import functools

import jax
import jax.numpy as jnp
from jax import lax
from jax.experimental import pallas as pl
from jax.experimental.pallas import tpu as pltpu
from jax.sharding import PartitionSpec as P

HEAD = 128
QUERIES = 256
SLOTS = 256
MESH = pl.DeviceIdType.MESH
INNER = 2
ALIGN = 16
AHEAD = 3


def greet(targets):
    barrier = pltpu.get_barrier_semaphore()
    for target in targets:
        pl.semaphore_signal(barrier, inc=1, device_id=target, device_id_type=MESH)
    pl.semaphore_wait(barrier, len(targets))


def push(src, dst, send_sem, recv_sem, target):
    copy = pltpu.make_async_remote_copy(
        src_ref=src, dst_ref=dst, send_sem=send_sem, recv_sem=recv_sem,
        device_id=target, device_id_type=MESH,
    )
    copy.start()
    return copy


def landed(ref, send_sem, recv_sem, target):
    pltpu.make_async_remote_copy(
        src_ref=ref, dst_ref=ref, send_sem=send_sem, recv_sem=recv_sem,
        device_id=target, device_id_type=MESH,
    ).wait_recv()


def gone(ref, send_sem, recv_sem, target):
    pltpu.make_async_remote_copy(
        src_ref=ref, dst_ref=ref, send_sem=send_sem, recv_sem=recv_sem,
        device_id=target, device_id_type=MESH,
    ).wait_send()


def place(outer, inner):
    me = lax.axis_index("mp")
    z, y = me // inner, me % inner
    partner = {"mp": z * inner + (1 - y)}
    ahead = [(z + 1 + k) % outer for k in range(outer - 1)]
    behind = [(z + outer - 1 - k) % outer for k in range(outer - 1)]
    return z, y, partner, ahead, behind


def encode_kernel(
    outer, rows, chunk, own_ref, gain_ref, w_in_ref, w_out_ref, out_ref,
    gathered, w_in_here, w_out_here, normed, total, parts, from_y, from_z, summed,
    in_sem, out_sem, local_sem, gzs, gzr, gys, gyr, rys, ryr, rzs, rzr, zs, zr, ys, yr, ps, pr,
):
    z, y, partner, ahead, behind = place(outer, INNER)
    n = outer * INNER
    chunks = w_in_here.shape[0]
    cuts = ryr.shape[1]
    cut = rows // cuts
    p = lax.axis_index("pass")
    twin = {"pass": 1 - p}

    def load_in(c):
        cols = pl.ds(pl.multiple_of(c * chunk, chunk), chunk)
        return pltpu.make_async_copy(w_in_ref.at[:, cols], w_in_here.at[c], in_sem.at[c])

    def load_out(c):
        cols = pl.ds(pl.multiple_of(c * chunk, chunk), chunk)
        return pltpu.make_async_copy(w_out_ref.at[cols, :], w_out_here.at[c], out_sem.at[c])

    for c in range(min(AHEAD, chunks)):
        load_in(c).start()
        load_out(c).start()
    greet([partner, twin] + [{"mp": zz * INNER + y} for zz in ahead])

    def start(zz, yy):
        return pl.multiple_of((zz * INNER + yy) * rows, rows)

    def held(zz, yy):
        return gathered.at[pl.ds(start(zz, yy), rows)]

    push(own_ref, held(z, y), gys.at[0], gyr.at[0], partner)
    for k in range(outer - 1):
        push(own_ref, held(z, y), gzs.at[k], gzr.at[k], {"mp": ahead[k] * INNER + y})
    local = pltpu.make_async_copy(own_ref, held(z, y), local_sem)
    local.start()
    local.wait()

    def add_pair(k):
        owner = (z + outer - k) % outer
        for i in range(cuts):
            at = pl.ds(i * cut, cut)
            landed(from_y.at[k, at], rys.at[k, i], ryr.at[k, i], partner)
            here = parts[k, pl.ds(pl.multiple_of(y * rows + i * cut, cut), cut), :]
            summed[k - 1, at, :] = (
                here.astype(jnp.float32) + from_y[k, at, :].astype(jnp.float32)
            ).astype(jnp.bfloat16)
            push(summed.at[k - 1, at], from_z.at[k - 1, at], rzs.at[k - 1, i],
                 rzr.at[k - 1, i], {"mp": owner * INNER + y})

    def group(k, carry):
        zz = (z + outer - k) % outer
        landed(held(zz, 1 - y), gys.at[k], gyr.at[k], partner)
        wide = gathered[pl.ds(start(zz, 0), INNER * rows), :].astype(jnp.float32)
        scale = lax.rsqrt(jnp.mean(wide * wide, axis=-1, keepdims=True) + 1e-06)
        normed[...] = (wide * scale * gain_ref[...]).astype(jnp.bfloat16)
        total[...] = jnp.zeros_like(total)

        def piece(c, carry):
            @pl.when(k == 0)
            def _():
                @pl.when(c + AHEAD < chunks)
                def _():
                    load_in(c + AHEAD).start()
                    load_out(c + AHEAD).start()

                load_in(c).wait()
                load_out(c).wait()

            hidden = jnp.maximum(
                jnp.dot(normed[...], w_in_here[c], preferred_element_type=jnp.float32), 0.0
            ).astype(jnp.bfloat16)
            total[...] += jnp.dot(hidden, w_out_here[c], preferred_element_type=jnp.float32)

            @pl.when((c == (chunks - 1) // 2) & (k < outer - 1))
            def _():
                later = held((z + outer - k - 1) % outer, y)
                landed(later, gzs.at[k], gzr.at[k], partner)
                push(later, later, gys.at[k + 1], gyr.at[k + 1], partner)

            @pl.when((c == (chunks - 1) // 2) & (k > 1))
            def _():
                add_pair(k - 1)

            return carry

        lax.fori_loop(0, chunks, piece, 0)
        parts[k] = total[...].astype(jnp.bfloat16)
        for i in range(cuts):
            away = pl.ds(pl.multiple_of((1 - y) * rows + i * cut, cut), cut)
            push(parts.at[k, away], from_y.at[k, pl.ds(i * cut, cut)], rys.at[k, i],
                 ryr.at[k, i], partner)
        return carry

    lax.fori_loop(0, outer, group, 0)
    add_pair(outer - 1)

    def block(pp, zz, yy, i):
        first = pp * n * rows + start(zz, yy) + i * cut
        return out_ref.at[pl.ds(pl.multiple_of(first, cut), cut)]

    def spread(zz, i):
        here = block(p, zz, y, i)
        at = zz * INNER + y
        push(here, here, ys.at[zz, i], yr.at[zz, i], partner)
        push(here, here, ps.at[at, i], pr.at[at, i], twin)

    def relay(zz, s, side, on, keep, i):
        @pl.when(keep)
        def _():
            here = block(p, zz, y, i)
            if s > 0:
                landed(here, zs.at[side, s - 1, i], zr.at[side, s - 1, i], partner)
            following = z + 1 if side == 0 else z - 1

            @pl.when(on)
            def _():
                push(here, here, zs.at[side, s, i], zr.at[side, s, i],
                     {"mp": following * INNER + y})

            if s > 0:
                spread(zz, i)

    upward, downward = z < outer - 1, z > 0
    for i in range(cuts):
        at = pl.ds(i * cut, cut)
        landed(from_y.at[0, at], rys.at[0, i], ryr.at[0, i], partner)
        mine = pl.ds(pl.multiple_of(y * rows + i * cut, cut), cut)
        ffn = parts[0, mine, :].astype(jnp.float32) + from_y[0, at, :].astype(jnp.float32)
        for k in range(outer - 1):
            landed(from_z.at[k, at], rzs.at[k, i], rzr.at[k, i], partner)
            ffn += from_z[k, at, :].astype(jnp.float32)
        own = pl.multiple_of(p * n * rows + start(z, y) + i * cut, cut)
        out_ref[pl.ds(own, cut), :] = (
            own_ref[at, :].astype(jnp.float32) + ffn
        ).astype(jnp.bfloat16)
        relay(z, 0, 0, upward, z >= 0, i)
        relay(z, 0, 1, downward, z >= 0, i)
        spread(z, i)
    for s in range(1, outer):
        for i in range(cuts):
            relay(z - s, s, 0, upward, z - s >= 0, i)
            relay(z + s, s, 1, downward, z + s < outer, i)

    def cross(zz, keep, i):
        @pl.when(keep)
        def _():
            here = block(p, zz, 1 - y, i)
            landed(here, ys.at[zz, i], yr.at[zz, i], partner)
            at = zz * INNER + 1 - y
            push(here, here, ps.at[at, i], pr.at[at, i], twin)

    for i in range(cuts):
        cross(z, z >= 0, i)
    for s in range(1, outer):
        for i in range(cuts):
            cross(z - s, z - s >= 0, i)
            cross(z + s, z + s < outer, i)
    for i in range(cuts):
        some = block(p, z, y, i)
        for k in range(n):
            landed(block(1 - p, k // INNER, k % INNER, i), ps.at[k, i], pr.at[k, i], twin)
            gone(some, ps.at[k, i], pr.at[k, i], twin)
        for k in range(outer):
            gone(some, ys.at[k, i], yr.at[k, i], partner)
            gone(some, rys.at[k, i], ryr.at[k, i], partner)

            @pl.when(upward & (z - k >= 0))
            def _():
                gone(some, zs.at[0, k, i], zr.at[0, k, i], partner)

            @pl.when(downward & (z + k < outer))
            def _():
                gone(some, zs.at[1, k, i], zr.at[1, k, i], partner)

        for k in range(outer - 1):
            gone(some, rzs.at[k, i], rzr.at[k, i], partner)
    for k in range(outer):
        gone(held(z, y), gys.at[k], gyr.at[k], partner)
    for k in range(outer - 1):
        gone(held(z, y), gzs.at[k], gzr.at[k], partner)


def encode(passages, gain, w_in, w_out, outer):
    rows, width = passages.shape
    n = outer * INNER
    units = w_in.shape[1]
    chunk = min(units, 1024)
    while units % chunk:
        chunk -= 128
    chunks = units // chunk
    cuts = 2 if rows % (2 * ALIGN) == 0 else 1
    dma = pltpu.SemaphoreType.DMA
    vmem = pl.BlockSpec(memory_space=pltpu.VMEM)
    hbm = pl.BlockSpec(memory_space=pl.ANY)
    bf16 = jnp.bfloat16
    return pl.pallas_call(
        functools.partial(encode_kernel, outer, rows, chunk),
        out_shape=jax.ShapeDtypeStruct((2 * n * rows, width), bf16),
        in_specs=[vmem, vmem, hbm, hbm],
        out_specs=vmem,
        scratch_shapes=[
            pltpu.VMEM((n * rows, width), bf16),
            pltpu.VMEM((chunks, width, chunk), bf16),
            pltpu.VMEM((chunks, chunk, width), bf16),
            pltpu.VMEM((INNER * rows, width), bf16),
            pltpu.VMEM((INNER * rows, width), jnp.float32),
            pltpu.VMEM((outer, INNER * rows, width), bf16),
            pltpu.VMEM((outer, rows, width), bf16),
            pltpu.VMEM((outer - 1, rows, width), bf16),
            pltpu.VMEM((outer - 1, rows, width), bf16),
            dma((chunks,)), dma((chunks,)), dma,
            dma((outer - 1,)), dma((outer - 1,)), dma((outer,)), dma((outer,)),
            dma((outer, cuts)), dma((outer, cuts)), dma((outer - 1, cuts)), dma((outer - 1, cuts)),
            dma((2, outer, cuts)), dma((2, outer, cuts)), dma((outer, cuts)), dma((outer, cuts)),
            dma((n, cuts)), dma((n, cuts)),
        ],
        compiler_params=pltpu.CompilerParams(
            collective_id=0, has_side_effects=True, vmem_limit_bytes=60 * 1024 * 1024
        ),
        name="encode",
    )(passages, gain[None, :], w_in, w_out)


def attend_kernel(
    counts_ref, ids_ref, rows_ref, wk_ref, wv_ref, q_ref, o_ref, slot_ref, key_ref, value_ref
):
    q = pl.program_id(1)
    first = pl.program_id(0) == 0
    questions = counts_ref.shape[0]
    offset, own_offset = [jnp.int32(0)], jnp.int32(0)
    for j in range(questions):
        room = (counts_ref[j] + ALIGN - 1) // ALIGN * ALIGN
        own_offset += jnp.where(j < q, room, 0)
        offset.append(offset[-1] + room)
    own_offset = pl.multiple_of(own_offset, ALIGN)

    @pl.when(q == 0)
    def _():
        tiles = (offset[questions] + SLOTS - 1) // SLOTS

        def tile(t, carry):
            here = pl.ds(pl.multiple_of(t * SLOTS, SLOTS), SLOTS)

            @pl.when(first)
            def _():
                ids = ids_ref[...]
                packed = jnp.full_like(ids, -1)
                for j in range(questions):
                    mine = (ids >= j * SLOTS) & (ids < (j + 1) * SLOTS)
                    packed = jnp.where(mine, ids - j * SLOTS + offset[j], packed)
                line = lax.broadcasted_iota(jnp.int32, (SLOTS, ids.shape[1]), 0) + t * SLOTS
                named = jnp.where(line == packed, 1.0, 0.0).astype(jnp.bfloat16)
                slot_ref[here, :] = jnp.dot(
                    named, rows_ref[...], preferred_element_type=jnp.float32
                ).astype(jnp.bfloat16)

            slots = slot_ref[here, :]
            key_ref[here, :] = jnp.dot(
                slots, wk_ref[...], preferred_element_type=jnp.float32
            ).astype(jnp.bfloat16)
            value_ref[here, :] = jnp.dot(
                slots, wv_ref[...], preferred_element_type=jnp.float32
            ).astype(jnp.bfloat16)
            return carry

        lax.fori_loop(0, tiles, tile, 0)
        tail = pl.ds(pl.multiple_of(tiles * SLOTS, SLOTS), SLOTS)
        value_ref[tail, :] = jnp.zeros((SLOTS, value_ref.shape[1]), jnp.bfloat16)

    def mix(width):
        valid = lax.broadcasted_iota(jnp.int32, (QUERIES, width), 1) < counts_ref[q]
        for h in range(wk_ref.shape[1] // HEAD):
            cols = slice(h * HEAD, (h + 1) * HEAD)
            scores = lax.dot_general(
                q_ref[0, :, cols], key_ref[pl.ds(own_offset, width), cols],
                (((1,), (1,)), ((), ())), preferred_element_type=jnp.float32,
            )
            scores = jnp.where(valid, scores, -1e30)
            peak = jnp.max(scores, axis=-1, keepdims=True)
            raised = jnp.exp(scores - peak)
            share = 1.0 / jnp.sum(raised, axis=-1, keepdims=True)
            o_ref[0, :, cols] = jnp.dot(
                (raised * share).astype(jnp.bfloat16),
                value_ref[pl.ds(own_offset, width), cols],
                preferred_element_type=jnp.float32,
            ).astype(jnp.bfloat16)

    few = counts_ref[q] <= SLOTS // 2

    @pl.when(few)
    def _():
        mix(SLOTS // 2)

    @pl.when(jnp.logical_not(few))
    def _():
        mix(SLOTS)


def attend(counts, shifted, all_rows, w_key, w_value, queries):
    questions, asked, cols = queries.shape
    total, width = all_rows.shape
    step = min(cols, 8 * HEAD)
    while cols % step:
        step -= HEAD
    return pl.pallas_call(
        attend_kernel,
        out_shape=jax.ShapeDtypeStruct(queries.shape, jnp.bfloat16),
        grid_spec=pltpu.PrefetchScalarGridSpec(
            num_scalar_prefetch=1,
            grid=(cols // step, questions),
            in_specs=[
                pl.BlockSpec((1, total), lambda c, q, s: (0, 0)),
                pl.BlockSpec((total, width), lambda c, q, s: (0, 0)),
                pl.BlockSpec((width, step), lambda c, q, s: (0, c)),
                pl.BlockSpec((width, step), lambda c, q, s: (0, c)),
                pl.BlockSpec((1, asked, step), lambda c, q, s: (q, 0, c)),
            ],
            out_specs=pl.BlockSpec((1, asked, step), lambda c, q, s: (q, 0, c)),
            scratch_shapes=[
                pltpu.VMEM((questions * SLOTS, width), jnp.bfloat16),
                pltpu.VMEM((questions * SLOTS + SLOTS, step), jnp.bfloat16),
                pltpu.VMEM((questions * SLOTS + SLOTS, step), jnp.bfloat16),
            ],
        ),
        compiler_params=pltpu.CompilerParams(vmem_limit_bytes=56 * 1024 * 1024),
        name="attend",
    )(counts, shifted, all_rows, w_key, w_value, queries)


def per_device(devices, passages, gain, w_in, w_out, w_key, w_value, queries, ids, counts):
    outer = devices // INNER
    all_rows = encode(passages, gain, w_in, w_out, outer)
    slot_total = counts.shape[0] * SLOTS
    shifted = (ids - lax.axis_index("pass") * slot_total)[None, :]
    return attend(counts, shifted, all_rows, w_key, w_value, queries)


def solution(mesh):
    placed = (
        P(("groups", "pass", "mp"), None),
        P(),
        P(None, "mp"),
        P("mp", None),
        P(None, "mp"),
        P(None, "mp"),
        P(("groups", "pass"), None, "mp"),
        P("groups"),
        P(("groups", "pass")),
    )
    return jax.shard_map(
        functools.partial(per_device, mesh.shape["mp"]),
        mesh=mesh,
        in_specs=placed,
        out_specs=P(("groups", "pass"), None, "mp"),
        check_vma=False,
    )
```
